32 devices in a mesh: rep: 4 (over y, x), dp: 8 (over z, core).
Axes of the slice: x: 2, y: 2, z: 4, core: 2. Of those that a mesh axis runs over, the one named last changes fastest.
Arguments:
- pixels: int32 [64, 144, 196], P(('rep', 'dp')), may hold values from 0 to 255
- return_ids: int32 [64, 4], P(('rep', 'dp')), may hold values from 0 to 119
- action_ids: int32 [64, 4], P(('rep', 'dp')), may hold values from 0 to 17
- reward_ids: int32 [64, 4], P(('rep', 'dp')), may hold values from 0 to 3
- type_map: int32 [64, 156], P(('rep', 'dp')), may hold values from 0 to 3, as said below
- expert_flags: int32 [64], P(('rep', 'dp')), may hold values 0 or 1
- inner_step: int32 [1], replicated, may hold values from 2 to 20
- attention_weight: float32 [4, 1792, 1792], P(None, 'dp')
- attention_drift: float32 [4, 4, 1792, 1792], P('rep', None, 'dp'), may hold values from -0.02734375 to 0.02734375
- attention_moment: float32 [4, 4, 1792, 1792], P('rep', None, 'dp'), may hold values from -0.00010681152 to 0.00010681152
- attention_square: float32 [4, 4, 1792, 1792], P('rep', None, 'dp'), may hold values from 1.3354959e-09 to 5.2915876e-09
- attention_velocity: float32 [4, 1792, 1792], P(None, 'dp'), may hold values from -0.0625 to 0.0625
- feedforward_weight: float32 [2, 1792, 7168], P(None, 'dp'), may hold values from -0.125 to 0.125
- feedforward_drift: float32 [4, 2, 1792, 7168], P('rep', None, 'dp'), may hold values from -0.02734375 to 0.02734375
- feedforward_moment: float32 [4, 2, 1792, 7168], P('rep', None, 'dp'), may hold values from -0.00010681152 to 0.00010681152
- feedforward_square: float32 [4, 2, 1792, 7168], P('rep', None, 'dp'), may hold values from 1.3354959e-09 to 5.2915876e-09
- feedforward_velocity: float32 [2, 1792, 7168], P(None, 'dp'), may hold values from -0.0625 to 0.0625
- embedding_weight: float32 [494, 1792], P(None, 'dp')
- embedding_drift: float32 [4, 494, 1792], P('rep', None, 'dp'), may hold values from -0.625 to 0.625
- embedding_moment: float32 [4, 494, 1792], P('rep', None, 'dp'), may hold values from -0.00010681152 to 0.00010681152
- embedding_square: float32 [4, 494, 1792], P('rep', None, 'dp'), may hold values from 1.3354959e-09 to 5.2915876e-09
- embedding_velocity: float32 [494, 1792], P(None, 'dp'), may hold values from -0.625 to 0.625
- readout_weight: float32 [142, 1792], P(None, 'dp'), may hold values from -0.25 to 0.25
- readout_drift: float32 [4, 142, 1792], P('rep', None, 'dp'), may hold values from -0.0546875 to 0.0546875
- readout_moment: float32 [4, 142, 1792], P('rep', None, 'dp'), may hold values from -0.0004272461 to 0.0004272461
- readout_square: float32 [4, 142, 1792], P('rep', None, 'dp'), may hold values from 2.141833e-08 to 8.567332e-08
- readout_velocity: float32 [142, 1792], P(None, 'dp'), may hold values from -0.125 to 0.125
- gains_weight: float32 [6, 1792], P(None, 'dp')
- gains_drift: float32 [4, 6, 1792], P('rep', None, 'dp'), may hold values from -0.625 to 0.625
- gains_moment: float32 [4, 6, 1792], P('rep', None, 'dp'), may hold values from -0.0008544922 to 0.0008544922
- gains_square: float32 [4, 6, 1792], P('rep', None, 'dp'), may hold values from 8.567332e-08 to 3.401735e-07
- gains_velocity: float32 [6, 1792], P(None, 'dp'), may hold values from -0.625 to 0.625
Outputs:
- loss: float32 [4], P('rep')
- gradient_norm: float32 [4], P('rep')
- updated_attention: float32 [4, 1792, 1792], P(None, 'dp')
- moment_attention: float32 [4, 4, 1792, 1792], P('rep', None, 'dp')
- square_attention: float32 [4, 4, 1792, 1792], P('rep', None, 'dp')
- velocity_attention: float32 [4, 1792, 1792], P(None, 'dp')
- updated_feedforward: float32 [2, 1792, 7168], P(None, 'dp')
- moment_feedforward: float32 [4, 2, 1792, 7168], P('rep', None, 'dp')
- square_feedforward: float32 [4, 2, 1792, 7168], P('rep', None, 'dp')
- velocity_feedforward: float32 [2, 1792, 7168], P(None, 'dp')
- updated_embedding: float32 [494, 1792], P(None, 'dp')
- moment_embedding: float32 [4, 494, 1792], P('rep', None, 'dp')
- square_embedding: float32 [4, 494, 1792], P('rep', None, 'dp')
- velocity_embedding: float32 [494, 1792], P(None, 'dp')
- updated_readout: float32 [142, 1792], P(None, 'dp')
- moment_readout: float32 [4, 142, 1792], P('rep', None, 'dp')
- square_readout: float32 [4, 142, 1792], P('rep', None, 'dp')
- velocity_readout: float32 [142, 1792], P(None, 'dp')
- updated_gains: float32 [6, 1792], P(None, 'dp')
- moment_gains: float32 [4, 6, 1792], P('rep', None, 'dp')
- square_gains: float32 [4, 6, 1792], P('rep', None, 'dp')
- velocity_gains: float32 [6, 1792], P(None, 'dp')
The draws below stay inside these ranges and needn't reach their ends.
Inputs may be any that keep to these rules, and one draw needn't show every extreme that they name: `type_map`: in each sequence the timesteps that carry marks are its last ones, one or more; such a timestep holds 1, 2, 3 at its positions 35, 36, 37; every other position holds 0.
All inputs are finite; a program needn't handle non-finite values. No bound on the sum of `expert_flags` on one device may be relied on, other than what follows from the above.
Results may differ from the reference program's by a relative error of at most 0.02.
Values may be sent and summed in bfloat16 or wider, within the bound.
No kernel may reach another device: no remote copies, remote signals or barrier semaphores. Data moves between devices by JAX's collectives and lax.ppermute only.
A program may use at most 704 MiB of HBM per device.

```python
import math
import jax
import jax.numpy as jnp
from jax import lax

D = 1792
FF = 7168
HEADS = 14
HEAD_DIM = 128
PATCH_PIXELS = 196
RETURN_BINS = 120
ACTION_BINS = 18
REWARD_BINS = 4
PATCHES = 36
TIMESTEPS = 4
SEQ_DEV = 2
SPAN = 39
LENGTH = 156
HEAD_ROWS = 142
EMB_ROWS = 494
SEQ_REP = 16
SEQS = 64
PTOTAL = 39685632
N_REP = 4


def draw_attention_weight(key, part):
    shape = (4, D, D)
    base = jax.random.normal(key, shape, jnp.float32)
    factors = jnp.array([1.0, 1.0, 1.0, 3.0], dtype=jnp.float32)[:, None, None] / math.sqrt(D)
    return base * factors


def draw_embedding_weight(key, part):
    shape = (EMB_ROWS, D)
    base = jax.random.normal(key, shape, jnp.float32)
    row_index = jnp.arange(EMB_ROWS, dtype=jnp.int32)[:, None]
    factors = jnp.where(row_index < PATCH_PIXELS, 1.0 / math.sqrt(PATCH_PIXELS), jnp.where(row_index < PATCH_PIXELS + HEAD_ROWS, 1.0, 0.5))
    return base * factors


def draw_gains_weight(key, part):
    shape = (6, D)
    feature = jnp.arange(D, dtype=jnp.float32)[None, :] / (D - 1.0)
    base = jax.random.normal(key, shape, jnp.float32)
    ramp = 0.5 + feature
    row_index = jnp.arange(6, dtype=jnp.int32)[:, None]
    return jnp.where(row_index % 2 == 0, ramp * (1.0 + 0.1 * base), 0.1 * base)


def draw_type_map(key, part):
    sequence = jnp.arange(SEQS, dtype=jnp.int32)
    place = sequence % SEQ_REP
    extra = jax.random.randint(key, (SEQS,), 0, 2, dtype=jnp.int32)
    live = jnp.minimum(TIMESTEPS, 1 + TIMESTEPS * place // SEQ_REP + extra)
    column = jnp.arange(LENGTH, dtype=jnp.int32)
    step_of = column // SPAN
    mark = column % SPAN - (PATCHES - 2)
    marked = (mark >= 1) & (mark <= 3)
    alive = step_of[None, :] >= TIMESTEPS - live[:, None]
    return jnp.where(marked[None, :] & alive, mark[None, :], 0).astype(jnp.int32)


def plant(result, key, smallest, high):
    longest = result.shape.index(max(result.shape))
    spots = []
    for shift in (0, 1):
        where = [jax.random.randint(jax.random.fold_in(key, axis), (), 0, length) for axis, length in enumerate(result.shape)]
        where[longest] = (where[longest] + shift) % result.shape[longest]
        spots.append(tuple(where))
    return result.at[spots[0]].set(smallest).at[spots[1]].set(high)


def block_levels(own_key, dims, pieces, least, top_value):
    level, own = 1.0, jax.random.fold_in(own_key, 6)
    for position, blocks in pieces:
        draws = jnp.exp(jax.random.uniform(jax.random.fold_in(own, position), (blocks,), jnp.float32, least / len(pieces), top_value / len(pieces)))
        level = level * jnp.repeat(draws, dims[position] // blocks).reshape([-1 if axis == position else 1 for axis in range(len(dims))])
    return level


def bell_draw(rng, shape, spread, bound, cuts=(), held_as=jnp.bfloat16):
    level = block_levels(rng, shape, cuts, -0.22, 0.18) if cuts else 1.0
    values = jax.random.normal(rng, shape, jnp.float32) * spread * level
    return jnp.minimum(jnp.maximum(values, -bound), bound).astype(held_as)


def setup_inputs(seed: int = 0) -> dict:
    splits = jax.random.split(jax.random.key(seed), 33)
    pixels = plant(jax.random.randint(splits[0], (SEQS, TIMESTEPS * PATCHES, PATCH_PIXELS), 0, 256), jax.random.fold_in(splits[0], 1), 0, 255).astype(jnp.int32)
    return_ids = plant(jax.random.randint(splits[1], (SEQS, TIMESTEPS), 0, RETURN_BINS), jax.random.fold_in(splits[1], 1), 0, RETURN_BINS - 1).astype(jnp.int32)
    action_ids = plant(jax.random.randint(splits[2], (SEQS, TIMESTEPS), 0, ACTION_BINS), jax.random.fold_in(splits[2], 1), 0, ACTION_BINS - 1).astype(jnp.int32)
    reward_ids = plant(jax.random.randint(splits[3], (SEQS, TIMESTEPS), 0, REWARD_BINS), jax.random.fold_in(splits[3], 1), 0, REWARD_BINS - 1).astype(jnp.int32)
    type_map = draw_type_map(jax.random.fold_in(splits[32], 71), 0)
    expert_flags = plant((jax.random.randint(splits[5], (SEQS,), 0, 2) < 1).astype(jnp.int32), jax.random.fold_in(splits[5], 1), 0, 1)
    inner_step = jax.random.randint(splits[6], (1,), 2, 21).astype(jnp.int32)
    attention_weight = draw_attention_weight(jax.random.fold_in(splits[32], 71), 0)
    attention_drift = bell_draw(splits[8], (N_REP, 4, D, D), (0.2 / D ** 0.5), 0.02734375, ((0, 4), (2, 8)), jnp.float32)
    attention_moment = bell_draw(splits[9], (N_REP, 4, D, D), (0.11 / PTOTAL ** 0.5), 0.00010681152, ((0, 4), (2, 8)), jnp.float32)
    attention_square = jnp.clip(jnp.exp(math.log(5.291587612532567e-09) - 1.3768156 * jax.random.uniform(splits[10], (N_REP, 4, D, D), jnp.float32) ** block_levels(splits[10], (N_REP, 4, D, D), ((0, 4), (2, 8)), -0.2, 0.2)), 1.3354959360611929e-09, 5.291587612532567e-09)
    attention_velocity = bell_draw(splits[11], (4, D, D), (0.5 / D ** 0.5), 0.0625, ((1, 8),), jnp.float32)
    feedforward_weight = bell_draw(splits[12], (2, D, FF), D ** -0.5, 0.125, ((1, 8),), jnp.float32)
    feedforward_drift = bell_draw(splits[13], (N_REP, 2, D, FF), (0.2 / D ** 0.5), 0.02734375, ((0, 4), (2, 8)), jnp.float32)
    feedforward_moment = bell_draw(splits[14], (N_REP, 2, D, FF), (0.11 / PTOTAL ** 0.5), 0.00010681152, ((0, 4), (2, 8)), jnp.float32)
    feedforward_square = jnp.clip(jnp.exp(math.log(5.291587612532567e-09) - 1.3768156 * jax.random.uniform(splits[15], (N_REP, 2, D, FF), jnp.float32) ** block_levels(splits[15], (N_REP, 2, D, FF), ((0, 4), (2, 8)), -0.2, 0.2)), 1.3354959360611929e-09, 5.291587612532567e-09)
    feedforward_velocity = bell_draw(splits[16], (2, D, FF), (0.5 / D ** 0.5), 0.0625, ((1, 8),), jnp.float32)
    embedding_weight = draw_embedding_weight(jax.random.fold_in(splits[32], 71), 0)
    embedding_drift = bell_draw(splits[18], (N_REP, EMB_ROWS, D), 0.1, 0.625, ((0, 4), (2, 8)), jnp.float32)
    embedding_moment = bell_draw(splits[19], (N_REP, EMB_ROWS, D), (0.11 / PTOTAL ** 0.5), 0.00010681152, ((0, 4), (2, 8)), jnp.float32)
    embedding_square = jnp.clip(jnp.exp(math.log(5.291587612532567e-09) - 1.3768156 * jax.random.uniform(splits[20], (N_REP, EMB_ROWS, D), jnp.float32) ** block_levels(splits[20], (N_REP, EMB_ROWS, D), ((0, 4), (2, 8)), -0.2, 0.2)), 1.3354959360611929e-09, 5.291587612532567e-09)
    embedding_velocity = bell_draw(splits[21], (EMB_ROWS, D), 0.1, 0.625, ((1, 8),), jnp.float32)
    readout_weight = bell_draw(splits[22], (HEAD_ROWS, D), (2.0 / D ** 0.5), 0.25, ((1, 8),), jnp.float32)
    readout_drift = bell_draw(splits[23], (N_REP, HEAD_ROWS, D), (0.4 / D ** 0.5), 0.0546875, ((0, 4), (2, 8)), jnp.float32)
    readout_moment = bell_draw(splits[24], (N_REP, HEAD_ROWS, D), (0.45 / PTOTAL ** 0.5), 0.0004272461, ((0, 4), (2, 8)), jnp.float32)
    readout_square = jnp.clip(jnp.exp(math.log(8.567332088205148e-08) - 1.3862944 * jax.random.uniform(splits[25], (N_REP, HEAD_ROWS, D), jnp.float32) ** block_levels(splits[25], (N_REP, HEAD_ROWS, D), ((0, 4), (2, 8)), -0.2, 0.2)), 2.141833022051287e-08, 8.567332088205148e-08)
    readout_velocity = bell_draw(splits[26], (HEAD_ROWS, D), (1.0 / D ** 0.5), 0.125, ((1, 8),), jnp.float32)
    gains_weight = draw_gains_weight(jax.random.fold_in(splits[32], 71), 0)
    gains_drift = bell_draw(splits[28], (N_REP, 6, D), 0.1, 0.625, ((0, 4), (2, 8)), jnp.float32)
    gains_moment = bell_draw(splits[29], (N_REP, 6, D), (0.9 / PTOTAL ** 0.5), 0.0008544922, ((0, 4), (2, 8)), jnp.float32)
    gains_square = jnp.clip(jnp.exp(math.log(3.401735000352346e-07) - 1.3789143 * jax.random.uniform(splits[30], (N_REP, 6, D), jnp.float32) ** block_levels(splits[30], (N_REP, 6, D), ((0, 4), (2, 8)), -0.2, 0.2)), 8.567332088205148e-08, 3.401735000352346e-07)
    gains_velocity = bell_draw(splits[31], (6, D), 0.1, 0.625, ((1, 8),), jnp.float32)
    return dict(pixels=pixels, return_ids=return_ids, action_ids=action_ids, reward_ids=reward_ids, type_map=type_map, expert_flags=expert_flags, inner_step=inner_step, attention_weight=attention_weight, attention_drift=attention_drift, attention_moment=attention_moment, attention_square=attention_square, attention_velocity=attention_velocity, feedforward_weight=feedforward_weight, feedforward_drift=feedforward_drift, feedforward_moment=feedforward_moment, feedforward_square=feedforward_square, feedforward_velocity=feedforward_velocity, embedding_weight=embedding_weight, embedding_drift=embedding_drift, embedding_moment=embedding_moment, embedding_square=embedding_square, embedding_velocity=embedding_velocity, readout_weight=readout_weight, readout_drift=readout_drift, readout_moment=readout_moment, readout_square=readout_square, readout_velocity=readout_velocity, gains_weight=gains_weight, gains_drift=gains_drift, gains_moment=gains_moment, gains_square=gains_square, gains_velocity=gains_velocity)


EPS_NORM = 1e-05
BETA_ONE = 0.9
BETA_TWO = 0.95
ADAM_EPS = 1e-08
CLIP = 1.0
OUTER_MOMENTUM = 0.9
OUTER_RATE = 0.7
RATES = (0.05, 0.05, 0.3, 0.1, 0.4)
DECAYS = (0.1, 0.1, 0.0, 0.1, 0.0)
NEGATIVE = -1e+30
HIGHEST = lax.Precision.HIGHEST

@jax.custom_vjp
def low(v):
    return lax.optimization_barrier(v.astype(jnp.bfloat16)).astype(jnp.float32)

@jax.custom_vjp
def low_back(v):
    return v

def low_keep(v):
    return (low(v), None)

def low_pass(kept, grad):
    return (grad,)

def back_keep(v):
    return (v, None)

def back_low(kept, grad):
    return (low(grad),)
low.defvjp(low_keep, low_pass)
low_back.defvjp(back_keep, back_low)

def layer_norm(values, gain, shift):
    centered = values - lax.optimization_barrier(jnp.mean(values, axis=-1, keepdims=True))
    variance = lax.optimization_barrier(jnp.mean(centered * centered, axis=-1, keepdims=True))
    return centered * lax.rsqrt(variance + EPS_NORM) * gain + shift

def gelu(values):
    return 0.5 * values * (1.0 + jnp.tanh(0.7978845608028654 * (values + 0.044715 * values * values * values)))

def block_loss(params, pixels, targets, scales):
    attention, feedforward, embedding, readout, gains = [low(weight) for weight in params]
    count = pixels.shape[0]
    pixel_rows = low(pixels.astype(jnp.float32) / 127.5 - 1.0).reshape(count * TIMESTEPS * PATCHES, PATCH_PIXELS)
    patches = low_back(jnp.dot(pixel_rows, embedding[:PATCH_PIXELS], precision=HIGHEST, preferred_element_type=jnp.float32))
    table = embedding[PATCH_PIXELS:PATCH_PIXELS + HEAD_ROWS]
    tokens = table[targets]
    stream = jnp.concatenate([patches.reshape(count, TIMESTEPS, PATCHES, D), tokens], axis=2).reshape(count, LENGTH, D)
    stream = stream + embedding[PATCH_PIXELS + HEAD_ROWS:]
    normed = low(layer_norm(stream, gains[0], gains[1]))
    triple = low_back(low(jnp.einsum('bld,hde->hble', normed, attention[:3], precision=HIGHEST)))
    queries, key_rows, value_rows = [triple[number].reshape(count, LENGTH, HEADS, HEAD_DIM) for number in range(3)]
    scores = low_back(jnp.einsum('bqhe,bkhe->bhqk', queries, key_rows, precision=HIGHEST) * (1.0 / HEAD_DIM ** 0.5))
    causal = jnp.arange(LENGTH)[:, None] >= jnp.arange(LENGTH)[None, :]
    scores = jnp.where(causal, scores, NEGATIVE)
    highest_score = lax.optimization_barrier(jnp.max(scores, axis=-1, keepdims=True))
    expos = jnp.exp(scores - highest_score)
    probs = expos / lax.optimization_barrier(jnp.sum(expos, axis=-1, keepdims=True))
    mixed = low_back(low(jnp.einsum('bhqk,bkhe->bqhe', low(probs), value_rows, precision=HIGHEST))).reshape(count, LENGTH, D)
    stream_one = stream + low_back(jnp.einsum('bld,de->ble', mixed, attention[3], precision=HIGHEST))
    normed_two = low(layer_norm(stream_one, gains[2], gains[3]))
    hidden = low_back(jnp.einsum('bld,df->blf', normed_two, feedforward[0], precision=HIGHEST))
    activated = low(gelu(hidden))
    stream_two = stream_one + low_back(jnp.einsum('blf,df->bld', activated, feedforward[1], precision=HIGHEST))
    final = low_back(low(layer_norm(stream_two, gains[4], gains[5])))
    picked = final.reshape(count, TIMESTEPS, SPAN, D)[:, :, PATCHES - 1:PATCHES + 2]
    logits = low_back(jnp.einsum('btjd,vd->btjv', picked, readout, precision=HIGHEST))
    columns = jnp.arange(HEAD_ROWS, dtype=jnp.int32)
    lower = jnp.array([0, RETURN_BINS, RETURN_BINS + ACTION_BINS], dtype=jnp.int32)
    upper = jnp.array([RETURN_BINS, RETURN_BINS + ACTION_BINS, HEAD_ROWS], dtype=jnp.int32)
    allowed = (columns[None, :] >= lower[:, None]) & (columns[None, :] < upper[:, None])
    masked = jnp.where(allowed, logits, NEGATIVE)
    highest_logit = lax.optimization_barrier(jnp.max(masked, axis=-1, keepdims=True))
    log_total = highest_logit[..., 0] + jnp.log(lax.optimization_barrier(jnp.sum(jnp.exp(masked - highest_logit), axis=-1)))
    chosen = lax.optimization_barrier(jnp.sum(jnp.where(columns == targets[..., None], logits, 0.0), axis=-1))
    return jnp.sum(scales * (log_total - chosen))

def replica_pass(local, pixels, return_ids, action_ids, reward_ids, type_map, expert_flags):
    count = pixels.shape[0]
    targets = jnp.stack([return_ids, action_ids + RETURN_BINS, reward_ids + RETURN_BINS + ACTION_BINS], axis=-1).astype(jnp.int32)
    marks = (type_map.reshape(count, TIMESTEPS, SPAN)[:, :, PATCHES - 1:PATCHES + 2] == jnp.arange(1, 4, dtype=jnp.int32)).astype(jnp.float32)
    boost = jnp.array([2.0, 0.0, 0.0], dtype=jnp.float32)
    weights = marks * (1.0 + boost * expert_flags.astype(jnp.float32)[:, None, None])
    denoms = lax.optimization_barrier(jnp.sum(weights, axis=(0, 1)))
    scales = weights / denoms
    block = 4 * SEQ_DEV
    blocks = count // block

    def split(values):
        return values.reshape((blocks, block) + values.shape[1:])

    def advance(carry, inputs):
        loss_sum, grads = carry
        pixel_block, target_block, scale_block = inputs
        value, pull = jax.vjp(lambda params: block_loss(params, pixel_block, target_block, scale_block), local)
        new_grads = pull(jnp.ones_like(value))[0]
        return ((loss_sum + value, jax.tree.map(jnp.add, grads, new_grads)), None)
    start = (jnp.zeros((), jnp.float32), jax.tree.map(jnp.zeros_like, local))
    (loss, grads), unused = lax.scan(advance, start, (split(pixels), split(targets), split(scales)))
    return (loss, grads)

def reference(pixels, return_ids, action_ids, reward_ids, type_map, expert_flags, inner_step, attention_weight, attention_drift, attention_moment, attention_square, attention_velocity, feedforward_weight, feedforward_drift, feedforward_moment, feedforward_square, feedforward_velocity, embedding_weight, embedding_drift, embedding_moment, embedding_square, embedding_velocity, readout_weight, readout_drift, readout_moment, readout_square, readout_velocity, gains_weight, gains_drift, gains_moment, gains_square, gains_velocity):
    shared = (attention_weight, feedforward_weight, embedding_weight, readout_weight, gains_weight)
    drifts = (attention_drift, feedforward_drift, embedding_drift, readout_drift, gains_drift)
    moments = (attention_moment, feedforward_moment, embedding_moment, readout_moment, gains_moment)
    squares = (attention_square, feedforward_square, embedding_square, readout_square, gains_square)
    velocities = (attention_velocity, feedforward_velocity, embedding_velocity, readout_velocity, gains_velocity)
    steps = inner_step[0].astype(jnp.float32)
    bias_one = 1.0 - jnp.power(jnp.float32(BETA_ONE), steps)
    bias_two = 1.0 - jnp.power(jnp.float32(BETA_TWO), steps)
    losses, norms, new_locals, new_moments, new_squares = ([], [], [], [], [])
    for replica in range(N_REP):
        first = replica * SEQ_REP
        last = first + SEQ_REP
        local = tuple((weight + drift[replica] for weight, drift in zip(shared, drifts)))
        loss, grads = replica_pass(local, pixels[first:last], return_ids[first:last], action_ids[first:last], reward_ids[first:last], type_map[first:last], expert_flags[first:last])
        norm = jnp.sqrt(sum((jnp.sum(grad * grad) for grad in grads)))
        factor = CLIP / jnp.maximum(norm, CLIP)
        locals_here, moments_here, squares_here = ([], [], [])
        for group_index in range(5):
            clipped = grads[group_index] * factor
            moment = BETA_ONE * moments[group_index][replica] + (1.0 - BETA_ONE) * clipped
            square = BETA_TWO * squares[group_index][replica] + (1.0 - BETA_TWO) * clipped * clipped
            update = moment / bias_one / (jnp.sqrt(square / bias_two) + ADAM_EPS) + DECAYS[group_index] * local[group_index]
            locals_here.append(local[group_index] - RATES[group_index] * update)
            moments_here.append(moment)
            squares_here.append(square)
        losses.append(loss)
        norms.append(norm)
        new_locals.append(locals_here)
        new_moments.append(moments_here)
        new_squares.append(squares_here)
    outputs = [jnp.stack(losses), jnp.stack(norms)]
    for group_index in range(5):
        averaged = sum((new_locals[replica][group_index] for replica in range(N_REP))) / N_REP
        delta = shared[group_index] - averaged
        velocity = OUTER_MOMENTUM * velocities[group_index] + delta
        updated = shared[group_index] - OUTER_RATE * (delta + OUTER_MOMENTUM * velocity)
        outputs.append(updated)
        outputs.append(jnp.stack([new_moments[replica][group_index] for replica in range(N_REP)]))
        outputs.append(jnp.stack([new_squares[replica][group_index] for replica in range(N_REP)]))
        outputs.append(velocity)
    return tuple(outputs)
```

```python
import jax
import jax.numpy as jnp
from jax import lax
from jax.sharding import PartitionSpec as P

D = 1792
FF = 7168
HEADS = 14
HEAD_DIM = 128
PATCH_PIXELS = 196
RETURN_BINS = 120
ACTION_BINS = 18
PATCHES = 36
TIMESTEPS = 4
SPAN = 39
LENGTH = 156
HEAD_ROWS = 142
PICKS = 3 * TIMESTEPS

EPS_NORM = 1e-05
BETA_ONE = 0.9
BETA_TWO = 0.95
ADAM_EPS = 1e-08
CLIP = 1.0
OUTER_MOMENTUM = 0.9
OUTER_RATE = 0.7
RATES = (0.05, 0.05, 0.3, 0.1, 0.4)
DECAYS = (0.1, 0.1, 0.0, 0.1, 0.0)
NEGATIVE = -1e30
SCALE = 1.0 / HEAD_DIM**0.5
F32 = jnp.float32
BF16 = jnp.bfloat16


def dot(spec, left, right):
    return jnp.einsum(spec, left, right, preferred_element_type=F32)


def gelu(values):
    return (
        0.5
        * values
        * (1.0 + jnp.tanh(0.7978845608028654 * (values + 0.044715 * values * values * values)))
    )


def gather_rows(piece):
    return lax.all_gather(piece, "dp", axis=0, tiled=True)


def gather_columns(piece):
    whole = lax.all_gather(piece, "dp", axis=0)
    return jnp.moveaxis(whole, 0, 1).reshape(piece.shape[0], -1)


def scatter_rows(partial):
    count = lax.axis_size("dp")
    parts = partial.astype(BF16).reshape((count, partial.shape[0] // count) + partial.shape[1:])
    mine = lax.all_to_all(parts, "dp", split_axis=0, concat_axis=0, tiled=True)
    return jnp.sum(mine.astype(F32), axis=0)


def scatter_columns(partial):
    count = lax.axis_size("dp")
    parts = partial.astype(BF16).reshape(partial.shape[0], count, partial.shape[1] // count)
    mine = lax.all_to_all(
        jnp.moveaxis(parts, 1, 0), "dp", split_axis=0, concat_axis=0, tiled=True
    )
    return jnp.sum(mine.astype(F32), axis=0)


def sum_rows(partial):
    return gather_rows(scatter_rows(partial).astype(BF16))


def norm_rows(values):
    centered = values - jnp.mean(values, axis=-1, keepdims=True)
    inverse = lax.rsqrt(jnp.mean(centered * centered, axis=-1, keepdims=True) + EPS_NORM)
    return centered * inverse, inverse


def norm_rows_back(scaled, inverse, gain, upstream):
    shaped = upstream * gain
    first = jnp.mean(shaped, axis=-1, keepdims=True)
    second = jnp.mean(shaped * scaled, axis=-1, keepdims=True)
    return inverse * (shaped - first - scaled * second)


def own_columns(values, width):
    return lax.dynamic_slice_in_dim(
        values, lax.axis_index("dp") * width, width, values.ndim - 1
    )


def swap_hidden(weight):
    count = lax.axis_size("dp")
    here = lax.axis_index("dp")
    piece = FF // count
    width = weight.shape[1]
    result = jnp.zeros((2, D, piece), weight.dtype)
    for step in range(count):
        peer = here ^ step
        block = lax.dynamic_slice_in_dim(weight, peer * piece, piece, 2)
        if step:
            block = lax.ppermute(block, "dp", [(i, i ^ step) for i in range(count)])
        result = lax.dynamic_update_slice_in_dim(result, block, peer * width, 1)
    return result


def shards(
    pixels,
    return_ids,
    action_ids,
    reward_ids,
    type_map,
    expert_flags,
    inner_step,
    attention_weight,
    attention_drift,
    attention_moment,
    attention_square,
    attention_velocity,
    feedforward_weight,
    feedforward_drift,
    feedforward_moment,
    feedforward_square,
    feedforward_velocity,
    embedding_weight,
    embedding_drift,
    embedding_moment,
    embedding_square,
    embedding_velocity,
    readout_weight,
    readout_drift,
    readout_moment,
    readout_square,
    readout_velocity,
    gains_weight,
    gains_drift,
    gains_moment,
    gains_square,
    gains_velocity,
):
    shared = (attention_weight, feedforward_weight, embedding_weight, readout_weight, gains_weight)
    drifts = (attention_drift, feedforward_drift, embedding_drift, readout_drift, gains_drift)
    moments = (attention_moment, feedforward_moment, embedding_moment, readout_moment, gains_moment)
    squares_old = (
        attention_square,
        feedforward_square,
        embedding_square,
        readout_square,
        gains_square,
    )
    velocities = (
        attention_velocity,
        feedforward_velocity,
        embedding_velocity,
        readout_velocity,
        gains_velocity,
    )
    attention_low, feedforward_low, embedding_low, readout_low, gains_low = (
        (weight + drift[0]).astype(BF16) for weight, drift in zip(shared, drifts)
    )
    count = pixels.shape[0]
    devices = lax.axis_size("dp")
    seqs = count * devices
    width = D // devices
    rows = seqs * PICKS
    here = lax.axis_index("dp")

    pixel_rows = (pixels.astype(F32) / 127.5 - 1.0).astype(BF16)
    targets = jnp.stack(
        [return_ids, action_ids + RETURN_BINS, reward_ids + RETURN_BINS + ACTION_BINS], axis=-1
    )
    marks = (
        type_map.reshape(count, TIMESTEPS, SPAN)[:, :, PATCHES - 1 : PATCHES + 2]
        == jnp.arange(1, 4, dtype=jnp.int32)
    ).astype(F32)
    boost = jnp.array([2.0, 0.0, 0.0], dtype=F32)
    weights = marks * (1.0 + boost * expert_flags.astype(F32)[:, None, None])
    labels = jnp.stack([targets.astype(BF16), weights.astype(BF16)], axis=-1)
    labels = jnp.pad(labels, ((0, 0), (0, 0), (0, 0), (0, PATCH_PIXELS - 2)))
    packed = jnp.concatenate(
        [pixel_rows.reshape(count, TIMESTEPS, PATCHES, PATCH_PIXELS), labels], axis=2
    ).reshape(count, LENGTH, PATCH_PIXELS)
    packed = gather_rows(packed)
    small_full = lax.all_gather(jnp.concatenate([readout_low, gains_low], axis=0), "dp", axis=0)
    small_full = jnp.moveaxis(small_full, 0, 1).reshape(HEAD_ROWS + 6, D)
    readout_full = small_full[:HEAD_ROWS]
    gains_full = small_full[HEAD_ROWS:].astype(F32)
    gains_own = gains_low.astype(F32)
    hidden_weights = swap_hidden(feedforward_low)

    labels = packed.reshape(seqs, TIMESTEPS, SPAN, PATCH_PIXELS)[:, :, PATCHES:, :2].astype(F32)
    targets = labels[..., 0].astype(jnp.int32).reshape(rows)
    weights = labels[..., 1].reshape(rows)
    token_target = jnp.where(
        jnp.arange(LENGTH) % SPAN >= PATCHES, packed[:, :, 0].astype(F32), -1.0
    )
    is_token = (jnp.arange(LENGTH) % SPAN >= PATCHES)[None, :, None]
    features = jnp.concatenate(
        [
            jnp.where(is_token, 0.0, packed.astype(F32)).astype(BF16),
            (token_target[..., None] == jnp.arange(HEAD_ROWS, dtype=F32)).astype(BF16),
            jnp.broadcast_to(jnp.eye(LENGTH, dtype=BF16), (seqs, LENGTH, LENGTH)),
        ],
        axis=-1,
    ).reshape(seqs * LENGTH, -1)
    stream = dot("tv,vd->td", features, embedding_low)

    own_mean = jnp.mean(stream, axis=-1)
    own_square = jnp.sum(jnp.square(stream - own_mean[:, None]), axis=-1)
    stats = lax.all_gather(jnp.stack([own_mean, own_square]), "dp", axis=0)
    mean = jnp.mean(stats[:, 0], axis=0)
    variance = (
        jnp.sum(stats[:, 1], axis=0) + width * jnp.sum(jnp.square(stats[:, 0] - mean), axis=0)
    ) / D
    inverse = lax.rsqrt(variance + EPS_NORM)[:, None]
    scaled = (stream - mean[:, None]) * inverse
    normed = (scaled * gains_own[0] + gains_own[1]).astype(BF16).reshape(seqs, LENGTH, width)

    def picked(values):
        grid = values.reshape(seqs, TIMESTEPS, SPAN, width)
        return grid[:, :, PATCHES - 1 : PATCHES + 2].reshape(rows, width)

    query_weight, key_weight, value_weight, output_weight = attention_low
    key_weight = key_weight.reshape(width, HEADS, HEAD_DIM)
    value_weight = value_weight.reshape(width, HEADS, HEAD_DIM)
    normed_picked = picked(normed)
    queries = sum_rows(dot("rd,de->re", normed_picked, query_weight))
    queries = queries.reshape(rows, HEADS, HEAD_DIM)

    def by_sequence(values):
        grid = values.reshape(HEADS, seqs, PICKS, values.shape[-1])
        return jnp.swapaxes(grid, 0, 1).reshape(seqs, HEADS * PICKS, -1)

    def by_head(values):
        grid = values.reshape(seqs, HEADS, PICKS, values.shape[-1])
        return jnp.swapaxes(grid, 0, 1).reshape(HEADS, rows, -1)

    reach = by_sequence(dot("rhe,dhe->hrd", queries, key_weight).astype(BF16))
    scores = scatter_rows(dot("sqd,skd->sqk", reach, normed)) * SCALE
    place = (
        SPAN * (jnp.arange(PICKS) // 3) + PATCHES - 1 + jnp.arange(PICKS) % 3
    )
    seen = jnp.tile(jnp.arange(LENGTH)[None, :] <= place[:, None], (HEADS, 1))
    scores = jnp.where(seen, scores, NEGATIVE)
    expos = jnp.exp(scores - jnp.max(scores, axis=-1, keepdims=True))
    probs = expos / jnp.sum(expos, axis=-1, keepdims=True)
    probs_all = gather_rows(probs.astype(BF16))
    blend = by_head(dot("sqk,skd->sqd", probs_all, normed).astype(BF16))
    mixed_part = dot("hrd,dhe->rhe", blend, value_weight).reshape(rows, D)
    mixed = scatter_columns(mixed_part).astype(BF16)
    branch = scatter_columns(dot("rd,de->re", mixed, output_weight))
    stream_one = gather_columns((picked(stream) + branch).astype(BF16)).astype(F32)

    scaled_one, inverse_one = norm_rows(stream_one)
    normed_two = (scaled_one * gains_full[2] + gains_full[3]).astype(BF16)
    hidden = dot("rd,df->rf", normed_two, hidden_weights[0])
    activated = gelu(hidden).astype(BF16)
    stream_two = stream_one + sum_rows(
        dot("rf,df->rd", activated, hidden_weights[1])
    ).astype(F32)
    scaled_two, inverse_two = norm_rows(stream_two)
    final = (scaled_two * gains_full[4] + gains_full[5]).astype(BF16)

    kinds = jnp.arange(rows) % 3
    kind_hits = (kinds[:, None] == jnp.arange(3)[None, :]).astype(F32)
    denoms = jnp.sum(weights[:, None] * kind_hits, axis=0)
    columns = jnp.arange(HEAD_ROWS, dtype=jnp.int32)
    lower = jnp.where(kinds == 0, 0, jnp.where(kinds == 1, RETURN_BINS, RETURN_BINS + ACTION_BINS))
    upper = jnp.where(
        kinds == 0, RETURN_BINS, jnp.where(kinds == 1, RETURN_BINS + ACTION_BINS, HEAD_ROWS)
    )
    allowed = (columns[None, :] >= lower[:, None]) & (columns[None, :] < upper[:, None])
    logits = dot("rd,vd->rv", final, readout_full)
    masked = jnp.where(allowed, logits, NEGATIVE)
    highest = jnp.max(masked, axis=-1, keepdims=True)
    expos = jnp.exp(masked - highest)
    totals = jnp.sum(expos, axis=-1, keepdims=True)
    onehot = (columns[None, :] == targets[:, None]).astype(F32)
    cross = highest[:, 0] + jnp.log(totals[:, 0]) - jnp.sum(onehot * logits, axis=-1)
    loss = jnp.sum(jnp.sum((weights * cross)[:, None] * kind_hits, axis=0) / denoms)
    scale = weights / jnp.sum(kind_hits * denoms, axis=-1)
    slope = (scale[:, None] * (expos / totals - onehot)).astype(BF16)
    readout_grad = dot("rv,rd->vd", slope, own_columns(final, width))
    final_grad = dot("rv,vd->rd", slope, readout_full).astype(BF16).astype(F32)

    shift_five = own_columns(jnp.sum(final_grad, axis=0), width)
    gain_five = own_columns(jnp.sum(final_grad * scaled_two, axis=0), width)
    grad_two = norm_rows_back(scaled_two, inverse_two, gains_full[4], final_grad)
    output_grad = grad_two.astype(BF16)
    activated_grad = dot("rd,df->rf", output_grad, hidden_weights[1])
    unused, gelu_pull = jax.vjp(gelu, hidden)
    hidden_grad = gelu_pull(activated_grad)[0].astype(BF16)
    normed_two_grad = sum_rows(dot("rf,df->rd", hidden_grad, hidden_weights[0])).astype(F32)
    unit_rows = lax.all_gather(jnp.stack([hidden_grad, activated]), "dp", axis=0)
    unit_rows = jnp.transpose(unit_rows, (1, 2, 0, 3)).reshape(2, rows, FF)
    feedforward_grad = jnp.stack(
        [
            dot("rd,rf->df", own_columns(normed_two, width), unit_rows[0]),
            dot("rd,rf->df", own_columns(output_grad, width), unit_rows[1]),
        ]
    )
    shift_three = own_columns(jnp.sum(normed_two_grad, axis=0), width)
    gain_three = own_columns(jnp.sum(normed_two_grad * scaled_one, axis=0), width)
    grad_one = grad_two + norm_rows_back(scaled_one, inverse_one, gains_full[2], normed_two_grad)
    branch_grad = grad_one.astype(BF16)

    output_proj_grad = dot("rd,re->de", mixed, branch_grad)
    mixed_grad = gather_columns(dot("re,de->rd", branch_grad, output_weight).astype(BF16))
    mixed_grad = mixed_grad.reshape(rows, HEADS, HEAD_DIM)
    blend_grad_heads = dot("rhe,dhe->hrd", mixed_grad, value_weight).astype(BF16)
    value_weight_grad = dot("hrd,rhe->dhe", blend, mixed_grad).reshape(width, D)
    blend_grad = by_sequence(blend_grad_heads)
    prob_grad = scatter_rows(dot("sqd,skd->sqk", blend_grad, normed))
    score_grad = probs * (prob_grad - jnp.sum(probs * prob_grad, axis=-1, keepdims=True))
    score_grad = gather_rows((score_grad * SCALE).astype(BF16))
    reach_grad = by_head(dot("sqk,skd->sqd", score_grad, normed).astype(BF16))
    query_grad = sum_rows(dot("hrd,dhe->rhe", reach_grad, key_weight).reshape(rows, D))
    key_weight_grad = dot("hrd,rhe->dhe", reach_grad, queries).reshape(width, D)
    query_weight_grad = dot("rd,re->de", normed_picked, query_grad)
    normed_grad = dot("sqk,sqd->skd", probs_all, blend_grad) + dot(
        "sqk,sqd->skd", score_grad, reach
    )
    through_query = dot("re,de->rd", query_grad, query_weight)

    def spread(values):
        grid = values.reshape(seqs, TIMESTEPS, 3, width)
        return jnp.pad(
            grid, ((0, 0), (0, 0), (PATCHES - 1, SPAN - PATCHES - 2), (0, 0))
        ).reshape(seqs * LENGTH, width)

    normed_grad = normed_grad.reshape(seqs * LENGTH, width) + spread(through_query)
    shift_one = jnp.sum(normed_grad, axis=0)
    gain_one = jnp.sum(normed_grad * scaled, axis=0)
    shaped = normed_grad * gains_own[0]
    sums = jnp.stack([jnp.sum(shaped, axis=-1), jnp.sum(shaped * scaled, axis=-1)])
    sums = jnp.sum(lax.all_gather(sums, "dp", axis=0), axis=0)[..., None] / D
    grad_zero = spread(own_columns(grad_one, width)) + inverse * (
        shaped - sums[0] - scaled * sums[1]
    )
    embedding_grad = dot("tv,td->vd", features, grad_zero.astype(BF16))
    attention_grad = jnp.stack(
        [query_weight_grad, key_weight_grad, value_weight_grad, output_proj_grad]
    )
    gains_grad = jnp.stack([gain_one, shift_one, gain_three, shift_three, gain_five, shift_five])

    grads = (attention_grad, feedforward_grad, embedding_grad, readout_grad, gains_grad)
    total_squares = lax.psum(sum((jnp.sum(grad * grad) for grad in grads)), "dp")
    gradient_norm = jnp.sqrt(total_squares)
    factor = CLIP / jnp.maximum(gradient_norm, CLIP)
    steps = inner_step[0].astype(F32)
    bias_one = 1.0 - jnp.power(F32(BETA_ONE), steps)
    bias_two = 1.0 - jnp.power(F32(BETA_TWO), steps)
    changes, new_moments, new_squares = ([], [], [])
    for group in range(5):
        clipped = grads[group] * factor
        moment = BETA_ONE * moments[group][0] + (1.0 - BETA_ONE) * clipped
        square = BETA_TWO * squares_old[group][0] + (1.0 - BETA_TWO) * clipped * clipped
        drift = drifts[group][0]
        update = moment / bias_one / (jnp.sqrt(square / bias_two) + ADAM_EPS) + DECAYS[group] * (
            shared[group] + drift
        )
        changes.append((RATES[group] * update - drift).astype(BF16))
        new_moments.append(moment)
        new_squares.append(square)
    summed = lax.psum(tuple(changes), "rep")
    replicas = lax.axis_size("rep")
    outputs = [loss[None], gradient_norm[None]]
    for group in range(5):
        delta = summed[group].astype(F32) / replicas
        velocity = OUTER_MOMENTUM * velocities[group] + delta
        updated = shared[group] - OUTER_RATE * (delta + OUTER_MOMENTUM * velocity)
        outputs.append(updated)
        outputs.append(new_moments[group][None])
        outputs.append(new_squares[group][None])
        outputs.append(velocity)
    return tuple(outputs)


def solution(mesh):
    placed = (
        P(("rep", "dp"), None, None),
        P(("rep", "dp"), None),
        P(("rep", "dp"), None),
        P(("rep", "dp"), None),
        P(("rep", "dp"), None),
        P(("rep", "dp")),
        P(),
        P(None, "dp", None),
        P("rep", None, "dp", None),
        P("rep", None, "dp", None),
        P("rep", None, "dp", None),
        P(None, "dp", None),
        P(None, "dp", None),
        P("rep", None, "dp", None),
        P("rep", None, "dp", None),
        P("rep", None, "dp", None),
        P(None, "dp", None),
        P(None, "dp"),
        P("rep", None, "dp"),
        P("rep", None, "dp"),
        P("rep", None, "dp"),
        P(None, "dp"),
        P(None, "dp"),
        P("rep", None, "dp"),
        P("rep", None, "dp"),
        P("rep", None, "dp"),
        P(None, "dp"),
        P(None, "dp"),
        P("rep", None, "dp"),
        P("rep", None, "dp"),
        P("rep", None, "dp"),
        P(None, "dp"),
    )
    return jax.shard_map(
        shards,
        mesh=mesh,
        in_specs=placed,
        out_specs=(
            P("rep"),
            P("rep"),
            P(None, "dp", None),
            P("rep", None, "dp", None),
            P("rep", None, "dp", None),
            P(None, "dp", None),
            P(None, "dp", None),
            P("rep", None, "dp", None),
            P("rep", None, "dp", None),
            P(None, "dp", None),
            P(None, "dp"),
            P("rep", None, "dp"),
            P("rep", None, "dp"),
            P(None, "dp"),
            P(None, "dp"),
            P("rep", None, "dp"),
            P("rep", None, "dp"),
            P(None, "dp"),
            P(None, "dp"),
            P("rep", None, "dp"),
            P("rep", None, "dp"),
            P(None, "dp"),
        ),
        check_vma=False,
    )
```

```python
import jax
import jax.numpy as jnp
from jax import lax
from jax.experimental import pallas as pl
from jax.experimental.pallas import tpu as pltpu
from jax.sharding import PartitionSpec as P

D = 1792
FF = 7168
HEADS = 14
HEAD_DIM = 128
PATCH_PIXELS = 196
RETURN_BINS = 120
ACTION_BINS = 18
PATCHES = 36
TIMESTEPS = 4
SPAN = 39
LENGTH = 156
PADDED = 160
HEAD_ROWS = 142
PICKS = 3 * TIMESTEPS

EPS_NORM = 1e-05
BETA_ONE = 0.9
BETA_TWO = 0.95
ADAM_EPS = 1e-08
CLIP = 1.0
OUTER_MOMENTUM = 0.9
OUTER_RATE = 0.7
RATES = (0.05, 0.05, 0.3, 0.1, 0.4)
DECAYS = (0.1, 0.1, 0.0, 0.1, 0.0)
NEGATIVE = -1e30
SCALE = 1.0 / HEAD_DIM**0.5
F32 = jnp.float32
BF16 = jnp.bfloat16


def dot(spec, left, right):
    return jnp.einsum(spec, left, right, preferred_element_type=F32)


def gelu(values):
    return (
        0.5
        * values
        * (1.0 + jnp.tanh(0.7978845608028654 * (values + 0.044715 * values * values * values)))
    )


def swap(value, step, axis="dp"):
    return lax.ppermute(value, axis, [(i, i ^ step) for i in range(lax.axis_size(axis))])


def chips():
    return lax.axis_size("dp") // 2


def still(value):
    return value


def gather_rows(piece, then=still):
    others = then([swap(piece, 2 * k) for k in range(1, chips())])
    same = jnp.concatenate([piece] + others, axis=0)
    return jnp.concatenate([same, swap(same, 1)], axis=0)


def scatter_rows(partial, then=still):
    half = partial.shape[0] // 2
    size = half // chips()
    pair = partial[:half] + swap(partial[half:].astype(BF16), 1).astype(F32)
    away = pair[size:].astype(BF16)
    others = then(
        [swap(away[(k - 1) * size : k * size], 2 * k) for k in range(1, chips())]
    )
    return sum((other.astype(F32) for other in others), pair[:size])


def sum_rows(partial, then=still):
    return gather_rows(scatter_rows(partial).astype(BF16), then)


def turn(values, step):
    count = lax.axis_size("dp")
    order = [2 * k for k in range(chips())] + [2 * k + 1 for k in range(chips())]
    bits = count.bit_length() - 1
    grid = values.reshape((2,) * bits + values.shape[1:])
    place = order.index(step)
    axes = [bits - 1 - b for b in range(bits) if place >> b & 1]
    return lax.rev(grid, axes).reshape(values.shape) if axes else values


def natural(values):
    count = lax.axis_size("dp")
    bits = count.bit_length() - 1
    here = lax.axis_index("dp")
    grid = values.reshape((2,) * bits + values.shape[1:])
    for b in range(bits - 1):
        axis = bits - 1 - b
        grid = jnp.where((here >> (b + 1)) & 1 == 1, lax.rev(grid, (axis,)), grid)
    grid = jnp.where(here & 1 == 1, lax.rev(grid, (0,)), grid)
    half = count // 2
    grid = grid.reshape((2, half) + values.shape[1:])
    return jnp.swapaxes(grid, 0, 1).reshape(values.shape)


def relative(values):
    count = lax.axis_size("dp")
    bits = count.bit_length() - 1
    here = lax.axis_index("dp")
    half = count // 2
    grid = values.reshape((half, 2) + values.shape[1:])
    grid = jnp.swapaxes(grid, 0, 1).reshape((2,) * bits + values.shape[1:])
    for b in range(bits - 1):
        axis = bits - 1 - b
        grid = jnp.where((here >> (b + 1)) & 1 == 1, lax.rev(grid, (axis,)), grid)
    grid = jnp.where(here & 1 == 1, lax.rev(grid, (0,)), grid)
    return grid.reshape(values.shape)


def split_rows(values):
    count = lax.axis_size("dp")
    return values.reshape((count, values.shape[0] // count) + values.shape[1:])


def gather_columns(piece, then=still):
    pieces = split_rows(piece)
    others = then([swap(pieces, 2 * k) for k in range(1, chips())])
    same = jnp.stack([pieces] + [turn(other, 2 * k + 2) for k, other in enumerate(others)])
    both = jnp.concatenate([same, turn_inner(swap(same, 1), 1)], axis=0)
    return jnp.moveaxis(natural(both), 0, 2).reshape(piece.shape[0], -1)


def turn_inner(values, step):
    return jnp.swapaxes(turn(jnp.swapaxes(values, 0, 1), step), 0, 1)


def scatter_columns(partial, then=still):
    count = lax.axis_size("dp")
    width = partial.shape[1] // count
    pieces = jnp.moveaxis(split_rows(partial).reshape(count, -1, count, width), 2, 0)
    pieces = relative(pieces.astype(BF16))
    half = chips()
    pair = pieces[:half].astype(F32) + turn_inner(swap(pieces[half:], 1), 1).astype(F32)
    away = pair[1:].astype(BF16)
    others = then([swap(away[k - 1], 2 * k) for k in range(1, half)])
    total = pair[0]
    for k, other in enumerate(others):
        total = total + turn(other, 2 * k + 2).astype(F32)
    return total.reshape(partial.shape[0], width)


def sum_tokens(values):
    count = lax.axis_size("dp")
    grid = jnp.swapaxes(values.reshape(values.shape[0], count, -1), 0, 1)
    grid = grid + turn(swap(grid, 1), 1)
    total = grid
    for k in range(1, chips()):
        total = total + turn(swap(grid, 2 * k), 2 * k)
    return jnp.swapaxes(total, 0, 1).reshape(values.shape)


def pairs(values):
    while len(values) > 1:
        values = [values[i] + values[i + 1] for i in range(0, len(values), 2)]
    return values[0]


def sum_scalar(value):
    value = value + swap(value, 1)
    return pairs([value] + [swap(value, 2 * k) for k in range(1, chips())])


def norm_tokens(mean, square, width, then=still):
    count = lax.axis_size("dp")
    grid = jnp.stack([mean, square], axis=0).reshape(2, count, -1).swapaxes(0, 1)
    other = turn(swap(grid, 1), 1)
    middle = 0.5 * (grid[:, 0] + other[:, 0])
    gap = grid[:, 0] - other[:, 0]
    square = grid[:, 1] + other[:, 1] + (0.5 * width) * gap * gap
    grid = jnp.stack([middle, square], axis=1)
    others = then([swap(grid, 2 * k) for k in range(1, chips())])
    pieces = [grid] + [turn(other, 2 * k + 2) for k, other in enumerate(others)]
    middle = sum(piece[:, 0] for piece in pieces) / chips()
    square = sum(
        piece[:, 1] + (2.0 * width) * jnp.square(piece[:, 0] - middle) for piece in pieces
    )
    return middle.reshape(-1), lax.rsqrt(square.reshape(-1) / D + EPS_NORM)


def norm_rows(values):
    centered = values - jnp.mean(values, axis=-1, keepdims=True)
    inverse = lax.rsqrt(jnp.mean(centered * centered, axis=-1, keepdims=True) + EPS_NORM)
    return centered * inverse, inverse


def norm_rows_back(scaled, inverse, gain, upstream):
    shaped = upstream * gain
    first = jnp.mean(shaped, axis=-1, keepdims=True)
    second = jnp.mean(shaped * scaled, axis=-1, keepdims=True)
    return inverse * (shaped - first - scaled * second)


def own_columns(values, width):
    return lax.dynamic_slice_in_dim(
        values, lax.axis_index("dp") * width, width, values.ndim - 1
    )


def relative_order():
    return [2 * k for k in range(chips())] + [2 * k + 1 for k in range(chips())]


PLAN = [
    [],
    [(0, 4), (0, 5), (0, 2)],
    [(0, 6)],
    [(0, 7), (0, 3), (0, 1)],
    [(1, 4)],
    [(1, 5), (1, 2)],
    [(1, 6), (1, 7), (1, 3), (1, 1)],
]


class Background:
    def __init__(self, weight, drift, plan):
        count = lax.axis_size("dp")
        steps = [(m, step) for m in (0, 1) for step in range(1, count)]
        known = [job for jobs in plan for job in jobs]
        rest = [job for job in steps if job not in known]
        self.plan = [[job for job in jobs if job in steps] for jobs in plan]
        self.plan[-1] += rest
        self.weight, self.drift = weight, drift
        self.width = weight.shape[1]
        self.piece = weight.shape[2] // count
        self.moving = []
        self.done = [((m, 0), self.block((m, 0))) for m in (0, 1)]

    def block(self, job):
        m, step = job
        first = (lax.axis_index("dp") ^ step) * self.piece
        size = (1, self.width, self.piece)
        spot = (m, 0, first)
        return (
            lax.dynamic_slice(self.weight, spot, size) + lax.dynamic_slice(self.drift, spot, size)
        )[0].astype(BF16)

    def __call__(self, value):
        jobs = self.plan.pop(0) if self.plan else []
        blocks = [self.block(job) for job in jobs]
        arrived = self.moving[:-2] if len(self.moving) > 2 else []
        staying = self.moving[len(arrived) :]
        value, self.weight, self.drift, blocks, ended = lax.optimization_barrier(
            (value, self.weight, self.drift, blocks, [block for _, block in arrived])
        )
        self.done += [(job, block) for (job, _), block in zip(arrived, ended)]
        self.moving = staying + [(job, swap(block, job[1])) for job, block in zip(jobs, blocks)]
        return value

    def result(self, matrix):
        here = lax.axis_index("dp")
        whole = jnp.zeros((D, self.piece), BF16)
        for (m, step), block in self.done + self.moving:
            if m == matrix:
                whole = lax.dynamic_update_slice_in_dim(
                    whole, block, (here ^ step) * self.width, 0
                )
        return whole


def inner_step_kernel(rate, decay, scalars, grad, moment, square, weight, drift, *rest):
    moment_out, square_out, change_out = rest[-3:]
    clipped = grad[...] * scalars[0]
    first = BETA_ONE * moment[...] + (1.0 - BETA_ONE) * clipped
    second = BETA_TWO * square[...] + (1.0 - BETA_TWO) * clipped * clipped
    moment_out[...] = first
    square_out[...] = second
    update = (first * scalars[1]) / (jnp.sqrt(second * scalars[2]) + ADAM_EPS)
    away = drift[...]
    change_out[...] = (rate * (update + decay * (weight[...] + away)) - away).astype(BF16)


def tall_rows(rows, columns):
    return next(
        size for size in (112, 56, 32, 16, 8, rows) if rows % size == 0 and size * columns <= 2**18
    )


def inner_update(scalars, grad, moment, square, weight, drift, rate, decay, matrix, before=None):
    matrices, rows, columns = weight.shape
    tall = tall_rows(rows, columns)
    block = pl.BlockSpec((1, tall, columns), lambda r: (matrix, r, 0))
    flat = pl.BlockSpec((tall, columns), lambda r: (r, 0))
    kept = list(before) if before else []
    return pl.pallas_call(
        lambda *refs: inner_step_kernel(
            rate,
            decay,
            refs[0],
            refs[1],
            *[ref.at[0] for ref in refs[2:6]],
            *[ref.at[0] for ref in refs[-3:]],
        ),
        grid=(rows // tall,),
        in_specs=[pl.BlockSpec(memory_space=pltpu.SMEM), flat]
        + [block] * 4
        + [pl.BlockSpec(memory_space=pl.ANY)] * len(kept),
        out_specs=[block, block, block if matrices > 2 else pl.BlockSpec((1, tall, columns), lambda r: (0, r, 0))],
        out_shape=[
            jax.ShapeDtypeStruct(weight.shape, F32),
            jax.ShapeDtypeStruct(weight.shape, F32),
            jax.ShapeDtypeStruct((matrices if matrices > 2 else 1, rows, columns), BF16),
        ],
        input_output_aliases={6 + place: place for place in range(len(kept))},
    )(scalars, grad, moment, square, weight, drift, *kept)


def outer_step_kernel(delta, velocity, weight, *rest):
    updated_out, velocity_out = rest[-2:]
    change = delta[...].astype(F32)
    speed = OUTER_MOMENTUM * velocity[...] + change
    velocity_out[...] = speed
    updated_out[...] = weight[...] - OUTER_RATE * (change + OUTER_MOMENTUM * speed)


def outer_update(delta, velocity, weight, first, before=None):
    matrices, rows, columns = delta.shape
    tall = tall_rows(rows, columns)
    block = pl.BlockSpec((1, tall, columns), lambda m, r: (m + first, r, 0))
    own = pl.BlockSpec((1, tall, columns), lambda m, r: (m, r, 0))
    kept = list(before) if before else []
    return pl.pallas_call(
        outer_step_kernel,
        grid=(matrices, rows // tall),
        in_specs=[own, block, block] + [pl.BlockSpec(memory_space=pl.ANY)] * len(kept),
        out_specs=[block, block],
        out_shape=[jax.ShapeDtypeStruct(weight.shape, F32)] * 2,
        input_output_aliases={3: 0, 4: 1} if kept else {},
    )(delta, velocity, weight, *kept)


def halve(values, axis, bit):
    size = values.shape[axis] // 2
    keep = lax.dynamic_slice_in_dim(values, bit * size, size, axis)
    give = lax.dynamic_slice_in_dim(values, (1 - bit) * size, size, axis)
    return keep, give


def join(own, other, axis, bit):
    return jnp.where(
        bit == 1,
        jnp.concatenate([other, own], axis=axis),
        jnp.concatenate([own, other], axis=axis),
    )


def mean_over_replicas(values, axis, steps):
    place = lax.axis_index("rep")
    current = values
    bits = [(place // step) % 2 for step in steps]
    for step, bit in zip(steps, bits):
        keep, give = halve(current, axis, bit)
        current = keep.astype(F32) + swap(give.astype(BF16), step, "rep").astype(F32)
    current = (current / lax.axis_size("rep")).astype(BF16)
    for step, bit in zip(reversed(steps), reversed(bits)):
        current = join(current, swap(current, step, "rep"), axis, bit)
    return current


def both_ways(values, axis, cut, steps):
    half = values.shape[cut] // 2
    first = lax.slice_in_dim(values, 0, half, axis=cut)
    second = lax.slice_in_dim(values, half, 2 * half, axis=cut)
    return jnp.concatenate(
        [mean_over_replicas(first, axis, steps), mean_over_replicas(second, axis, steps[::-1])],
        axis=cut,
    )


def shards(
    pixels,
    return_ids,
    action_ids,
    reward_ids,
    type_map,
    expert_flags,
    inner_step,
    attention_weight,
    attention_drift,
    attention_moment,
    attention_square,
    attention_velocity,
    feedforward_weight,
    feedforward_drift,
    feedforward_moment,
    feedforward_square,
    feedforward_velocity,
    embedding_weight,
    embedding_drift,
    embedding_moment,
    embedding_square,
    embedding_velocity,
    readout_weight,
    readout_drift,
    readout_moment,
    readout_square,
    readout_velocity,
    gains_weight,
    gains_drift,
    gains_moment,
    gains_square,
    gains_velocity,
):
    shared = (attention_weight, feedforward_weight, embedding_weight, readout_weight, gains_weight)
    drifts = (attention_drift, feedforward_drift, embedding_drift, readout_drift, gains_drift)
    moments = (attention_moment, feedforward_moment, embedding_moment, readout_moment, gains_moment)
    squares_old = (
        attention_square,
        feedforward_square,
        embedding_square,
        readout_square,
        gains_square,
    )
    velocities = (
        attention_velocity,
        feedforward_velocity,
        embedding_velocity,
        readout_velocity,
        gains_velocity,
    )
    attention_low, embedding_low, readout_low, gains_low = (
        (shared[group] + drifts[group][0]).astype(BF16) for group in (0, 2, 3, 4)
    )
    count = pixels.shape[0]
    devices = lax.axis_size("dp")
    seqs = count * devices
    width = D // devices
    rows = seqs * PICKS
    here = lax.axis_index("dp")

    lanes = 2 * HEAD_DIM
    pixel_rows = (pixels.astype(F32) / 127.5 - 1.0).astype(BF16)
    targets = jnp.stack(
        [return_ids, action_ids + RETURN_BINS, reward_ids + RETURN_BINS + ACTION_BINS], axis=-1
    )
    marks = (
        type_map.reshape(count, TIMESTEPS, SPAN)[:, :, PATCHES - 1 : PATCHES + 2]
        == jnp.arange(1, 4, dtype=jnp.int32)
    ).astype(F32)
    boost = jnp.array([2.0, 0.0, 0.0], dtype=F32)
    weights = marks * (1.0 + boost * expert_flags.astype(F32)[:, None, None])
    labels = jnp.stack([targets.astype(BF16), weights.astype(BF16)], axis=-1)
    labels = jnp.pad(labels, ((0, 0), (0, 0), (0, 0), (PATCH_PIXELS, lanes - PATCH_PIXELS - 2)))
    pixel_rows = jnp.pad(pixel_rows, ((0, 0), (0, 0), (0, lanes - PATCH_PIXELS)))
    packed = jnp.concatenate(
        [pixel_rows.reshape(count, TIMESTEPS, PATCHES, lanes), labels], axis=2
    ).reshape(count, LENGTH, lanes)
    packed = jnp.pad(packed, ((0, 0), (0, PADDED - LENGTH), (0, 0)))
    background = Background(
        feedforward_weight,
        feedforward_drift[0],
        PLAN,
    )
    packed = background(packed)
    packed = gather_rows(packed, background)
    small = gather_rows(jnp.concatenate([readout_low, gains_low], axis=0)[None])
    small_full = jnp.moveaxis(natural(small), 0, 1).reshape(HEAD_ROWS + 6, D)
    readout_full = small_full[:HEAD_ROWS]
    gains_full = small_full[HEAD_ROWS:].astype(F32)
    gains_own = gains_low.astype(F32)

    labels = packed[:, :LENGTH].reshape(seqs, TIMESTEPS, SPAN, lanes)
    labels = labels[:, :, PATCHES:, PATCH_PIXELS : PATCH_PIXELS + 2]
    targets = labels[..., 0].astype(jnp.int32).reshape(rows)
    weights = labels[..., 1].astype(F32).reshape(rows)
    spots = jnp.arange(PADDED, dtype=jnp.int32)
    token_target = jnp.where(
        ((spots % SPAN >= PATCHES) & (spots < LENGTH))[None, :, None],
        packed[:, :, PATCH_PIXELS : PATCH_PIXELS + 1].astype(jnp.int32),
        -1,
    )
    table_rows = jnp.arange(HEAD_ROWS + LENGTH, dtype=jnp.int32)
    picks = (table_rows == token_target) | (table_rows - HEAD_ROWS == spots[:, None])
    picks = picks.astype(BF16).reshape(seqs * PADDED, -1)
    packed = packed.reshape(seqs * PADDED, lanes)
    patch_weight = jnp.pad(embedding_low[:PATCH_PIXELS], ((0, lanes - PATCH_PIXELS), (0, 0)))
    stream = dot("tp,pd->td", packed, patch_weight) + dot(
        "tv,vd->td", picks, embedding_low[PATCH_PIXELS:]
    )

    own_mean = jnp.mean(stream, axis=-1)
    own_square = jnp.sum(jnp.square(stream - own_mean[:, None]), axis=-1)
    mean, inverse = norm_tokens(own_mean, own_square, width, background)
    inverse = inverse[:, None]
    scaled = (stream - mean[:, None]) * inverse
    normed = (scaled * gains_own[0] + gains_own[1]).astype(BF16).reshape(seqs, PADDED, width)
    place = SPAN * (jnp.arange(PICKS) // 3) + PATCHES - 1 + jnp.arange(PICKS) % 3
    selector = (place[:, None] == spots[None, :]).astype(BF16)

    query_weight, key_weight, value_weight, output_weight = attention_low
    key_weight = key_weight.reshape(width, HEADS, HEAD_DIM)
    value_weight = value_weight.reshape(width, HEADS, HEAD_DIM)
    normed_picked = dot("jk,skd->sjd", selector, normed).astype(BF16).reshape(rows, width)
    queries = sum_rows(dot("rd,de->re", normed_picked, query_weight), background)
    queries = queries.reshape(rows, HEADS, HEAD_DIM)

    def by_sequence(values):
        grid = values.reshape(HEADS, seqs, PICKS, values.shape[-1])
        return jnp.swapaxes(grid, 0, 1).reshape(seqs, HEADS * PICKS, -1)

    def by_head(values):
        grid = values.reshape(seqs, HEADS, PICKS, values.shape[-1])
        return jnp.swapaxes(grid, 0, 1).reshape(HEADS, rows, -1)

    reach = by_sequence(dot("rhe,dhe->hrd", queries, key_weight).astype(BF16))
    scores = scatter_rows(dot("sqd,skd->sqk", reach, normed), background) * SCALE
    seen = jnp.tile(spots[None, :] <= place[:, None], (HEADS, 1))
    scores = jnp.where(seen, scores, NEGATIVE)
    expos = jnp.exp(scores - jnp.max(scores, axis=-1, keepdims=True))
    probs = expos / jnp.sum(expos, axis=-1, keepdims=True)
    probs_all = gather_rows(probs.astype(BF16), background)
    blend = by_head(dot("sqk,skd->sqd", probs_all, normed).astype(BF16))
    mixed_part = dot("hrd,dhe->rhe", blend, value_weight).reshape(rows, D)
    mixed = scatter_columns(mixed_part, background).astype(BF16)
    branch_part = dot("rd,de->re", mixed, output_weight)
    picked_stream = stream.reshape(seqs, PADDED, width)[:, :LENGTH]
    picked_stream = picked_stream.reshape(seqs, TIMESTEPS, SPAN, width)
    picked_stream = picked_stream[:, :, PATCHES - 1 : PATCHES + 2].reshape(rows, width)
    own = own_columns(branch_part, width) + picked_stream
    branch_part = lax.dynamic_update_slice_in_dim(branch_part, own, here * width, 1)
    stream_one = sum_rows(branch_part).astype(F32)
    up_weight = background.result(0)
    down_weight = background.result(1)

    scaled_one, inverse_one = norm_rows(stream_one)
    normed_two = (scaled_one * gains_full[2] + gains_full[3]).astype(BF16)
    hidden = dot("rd,df->rf", normed_two, up_weight)
    activated = gelu(hidden).astype(BF16)

    def by_device(values):
        return natural(split_rows(values))

    held = by_device(activated)

    def release(arrived):
        nonlocal held
        arrived, held = lax.optimization_barrier((arrived, held))
        return arrived

    stream_two = stream_one + sum_rows(
        dot("rf,df->rd", activated, down_weight), release
    ).astype(F32)
    activated_all = gather_rows(held[None])
    scaled_two, inverse_two = norm_rows(stream_two)
    final = (scaled_two * gains_full[4] + gains_full[5]).astype(BF16)

    kinds = jnp.arange(rows) % 3
    kind_hits = (kinds[:, None] == jnp.arange(3)[None, :]).astype(F32)
    denoms = jnp.sum(weights[:, None] * kind_hits, axis=0)
    columns = jnp.arange(HEAD_ROWS, dtype=jnp.int32)
    lower = jnp.where(kinds == 0, 0, jnp.where(kinds == 1, RETURN_BINS, RETURN_BINS + ACTION_BINS))
    upper = jnp.where(
        kinds == 0, RETURN_BINS, jnp.where(kinds == 1, RETURN_BINS + ACTION_BINS, HEAD_ROWS)
    )
    allowed = (columns[None, :] >= lower[:, None]) & (columns[None, :] < upper[:, None])
    logits = dot("rd,vd->rv", final, readout_full)
    masked = jnp.where(allowed, logits, NEGATIVE)
    highest = jnp.max(masked, axis=-1, keepdims=True)
    expos = jnp.exp(masked - highest)
    totals = jnp.sum(expos, axis=-1, keepdims=True)
    onehot = (columns[None, :] == targets[:, None]).astype(F32)
    cross = highest[:, 0] + jnp.log(totals[:, 0]) - jnp.sum(onehot * logits, axis=-1)
    scale = weights / jnp.sum(kind_hits * denoms, axis=-1)
    piece_loss = jnp.sum((scale * cross).reshape(devices, -1), axis=1)
    loss = pairs([piece_loss[i] for i in range(devices)])
    slope = (scale[:, None] * (expos / totals - onehot)).astype(BF16)
    readout_grad = dot("rv,rd->vd", slope, own_columns(final, width))
    final_grad = dot("rv,vd->rd", slope, readout_full).astype(BF16).astype(F32)

    shift_five = own_columns(jnp.sum(final_grad, axis=0), width)
    gain_five = own_columns(jnp.sum(final_grad * scaled_two, axis=0), width)
    grad_two = norm_rows_back(scaled_two, inverse_two, gains_full[4], final_grad)
    output_grad = grad_two.astype(BF16)
    activated_grad = dot("rd,df->rf", output_grad, down_weight)
    unused, gelu_pull = jax.vjp(gelu, hidden)
    hidden_grad = gelu_pull(activated_grad)[0].astype(BF16)
    held = by_device(hidden_grad)
    normed_two_grad = sum_rows(dot("rf,df->rd", hidden_grad, up_weight), release).astype(F32)
    hidden_grad_all = gather_rows(held[None])

    def unit_grad(left, pieces):
        whole = jnp.zeros((width, FF), F32)
        left = by_device(left).reshape(rows, width)
        for place, step in enumerate(relative_order()):
            piece = dot("rd,rf->df", left, pieces[place].reshape(rows, -1))
            whole = lax.dynamic_update_slice_in_dim(
                whole, piece, (here ^ step) * piece.shape[1], 1
            )
        return whole

    up_grad = unit_grad(own_columns(normed_two, width), hidden_grad_all)
    down_grad = unit_grad(own_columns(output_grad, width), activated_all)
    shift_three = own_columns(jnp.sum(normed_two_grad, axis=0), width)
    gain_three = own_columns(jnp.sum(normed_two_grad * scaled_one, axis=0), width)
    grad_one = grad_two + norm_rows_back(scaled_one, inverse_one, gains_full[2], normed_two_grad)
    branch_grad = grad_one.astype(BF16)

    output_proj_grad = dot("rd,re->de", mixed, branch_grad)
    mixed_grad = gather_columns(dot("re,de->rd", branch_grad, output_weight).astype(BF16))
    mixed_grad = mixed_grad.reshape(rows, HEADS, HEAD_DIM)
    blend_grad_heads = dot("rhe,dhe->hrd", mixed_grad, value_weight).astype(BF16)
    value_weight_grad = dot("hrd,rhe->dhe", blend, mixed_grad).reshape(width, D)
    blend_grad = by_sequence(blend_grad_heads)
    prob_grad = scatter_rows(dot("sqd,skd->sqk", blend_grad, normed))
    score_grad = probs * (prob_grad - jnp.sum(probs * prob_grad, axis=-1, keepdims=True))
    score_grad = gather_rows((score_grad * SCALE).astype(BF16))
    reach_grad = by_head(dot("sqk,skd->sqd", score_grad, normed).astype(BF16))
    query_grad = sum_rows(dot("hrd,dhe->rhe", reach_grad, key_weight).reshape(rows, D))
    key_weight_grad = dot("hrd,rhe->dhe", reach_grad, queries).reshape(width, D)
    query_weight_grad = dot("rd,re->de", normed_picked, query_grad)
    through_query = dot("re,de->rd", query_grad, query_weight).astype(BF16)

    def spread(values):
        return dot("jk,sjd->skd", selector, values.reshape(seqs, PICKS, width))

    normed_grad = (
        dot("sqk,sqd->skd", probs_all, blend_grad)
        + dot("sqk,sqd->skd", score_grad, reach)
        + spread(through_query)
    ).reshape(seqs * PADDED, width)
    shift_one = jnp.sum(normed_grad, axis=0)
    gain_one = jnp.sum(normed_grad * scaled, axis=0)
    shaped = normed_grad * gains_own[0]
    sums = jnp.stack([jnp.sum(shaped, axis=-1), jnp.sum(shaped * scaled, axis=-1)])
    sums = sum_tokens(sums)[..., None] / D
    residual = spread(own_columns(branch_grad, width)).reshape(seqs * PADDED, width)
    grad_zero = (residual + inverse * (shaped - sums[0] - scaled * sums[1])).astype(BF16)
    embedding_grad = jnp.concatenate(
        [
            dot("tp,td->pd", packed, grad_zero)[:PATCH_PIXELS],
            dot("tv,td->vd", picks, grad_zero),
        ]
    )
    gains_grad = jnp.stack([gain_one, shift_one, gain_three, shift_three, gain_five, shift_five])

    attention_grads = (query_weight_grad, key_weight_grad, value_weight_grad, output_proj_grad)
    grads = attention_grads + (up_grad, down_grad, embedding_grad, readout_grad, gains_grad)
    total_squares = sum_scalar(sum((jnp.sum(grad * grad) for grad in grads)))
    gradient_norm = jnp.sqrt(total_squares)
    factor = CLIP / jnp.maximum(gradient_norm, CLIP)
    steps = inner_step[0].astype(F32)
    bias_one = 1.0 - jnp.power(F32(BETA_ONE), steps)
    bias_two = 1.0 - jnp.power(F32(BETA_TWO), steps)
    scalars = jnp.stack([factor, 1.0 / bias_one, 1.0 / bias_two])
    new_moments, new_squares = ([None] * 5, [None] * 5)

    def small_step(group, grad):
        clipped = grad * factor
        moment = BETA_ONE * moments[group][0] + (1.0 - BETA_ONE) * clipped
        square = BETA_TWO * squares_old[group][0] + (1.0 - BETA_TWO) * clipped * clipped
        drift = drifts[group][0]
        update = moment / bias_one / (jnp.sqrt(square / bias_two) + ADAM_EPS) + DECAYS[group] * (
            shared[group] + drift
        )
        new_moments[group] = moment
        new_squares[group] = square
        return (RATES[group] * update - drift).astype(BF16)

    def big_step(group, matrix, grad, before=None):
        return inner_update(
            scalars,
            grad,
            moments[group][0],
            squares_old[group][0],
            shared[group],
            drifts[group][0],
            RATES[group],
            DECAYS[group],
            matrix,
            before,
        )

    before = None
    for matrix, grad in enumerate(attention_grads):
        before = big_step(0, matrix, grad, before)
    new_moments[0], new_squares[0], attention_change = before
    up_grad, attention_change = lax.optimization_barrier((up_grad, attention_change))
    *before, up_change = big_step(1, 0, up_grad)
    down_grad, up_change = lax.optimization_barrier((down_grad, up_change))
    new_moments[1], new_squares[1], down_change = big_step(1, 1, down_grad, before)
    replicas = lax.axis_size("rep")
    exchange = [1 << b for b in range(replicas.bit_length() - 1)]
    attention_delta = both_ways(attention_change, 0, 2, exchange)
    up_delta = both_ways(up_change, 2, 1, exchange)
    down_delta = both_ways(down_change, 2, 1, exchange)
    small_changes = jnp.concatenate(
        [small_step(2, embedding_grad), small_step(3, readout_grad), small_step(4, gains_grad)]
    )
    others = [small_changes] + [swap(small_changes, step, "rep") for step in range(1, replicas)]
    small_delta = pairs([other.astype(F32) for other in others]) / replicas

    finished = {0: outer_update(attention_delta, velocities[0], shared[0], 0)}
    before = outer_update(up_delta, velocities[1], shared[1], 0)
    finished[1] = outer_update(down_delta, velocities[1], shared[1], 1, before)
    outputs = [loss[None], gradient_norm[None]]
    bound = 0
    for group in range(5):
        if group in finished:
            updated, velocity = finished[group]
        else:
            delta = small_delta[bound : bound + shared[group].shape[0]]
            bound += shared[group].shape[0]
            velocity = OUTER_MOMENTUM * velocities[group] + delta
            updated = shared[group] - OUTER_RATE * (delta + OUTER_MOMENTUM * velocity)
        outputs.append(updated)
        outputs.append(new_moments[group][None])
        outputs.append(new_squares[group][None])
        outputs.append(velocity)
    return tuple(outputs)


def solution(mesh):
    placed = (
        P(("rep", "dp"), None, None),
        P(("rep", "dp"), None),
        P(("rep", "dp"), None),
        P(("rep", "dp"), None),
        P(("rep", "dp"), None),
        P(("rep", "dp")),
        P(),
        P(None, "dp", None),
        P("rep", None, "dp", None),
        P("rep", None, "dp", None),
        P("rep", None, "dp", None),
        P(None, "dp", None),
        P(None, "dp", None),
        P("rep", None, "dp", None),
        P("rep", None, "dp", None),
        P("rep", None, "dp", None),
        P(None, "dp", None),
        P(None, "dp"),
        P("rep", None, "dp"),
        P("rep", None, "dp"),
        P("rep", None, "dp"),
        P(None, "dp"),
        P(None, "dp"),
        P("rep", None, "dp"),
        P("rep", None, "dp"),
        P("rep", None, "dp"),
        P(None, "dp"),
        P(None, "dp"),
        P("rep", None, "dp"),
        P("rep", None, "dp"),
        P("rep", None, "dp"),
        P(None, "dp"),
    )
    return jax.shard_map(
        shards,
        mesh=mesh,
        in_specs=placed,
        out_specs=(
            P("rep"),
            P("rep"),
            P(None, "dp", None),
            P("rep", None, "dp", None),
            P("rep", None, "dp", None),
            P(None, "dp", None),
            P(None, "dp", None),
            P("rep", None, "dp", None),
            P("rep", None, "dp", None),
            P(None, "dp", None),
            P(None, "dp"),
            P("rep", None, "dp"),
            P("rep", None, "dp"),
            P(None, "dp"),
            P(None, "dp"),
            P("rep", None, "dp"),
            P("rep", None, "dp"),
            P(None, "dp"),
            P(None, "dp"),
            P("rep", None, "dp"),
            P("rep", None, "dp"),
            P(None, "dp"),
        ),
        check_vma=False,
    )
```
